32 devices in a mesh: dates: 2 (over y), ctx: 16 (over z, x, core).
Axes of the slice: x: 2, y: 2, z: 4, core: 2. Of those that a mesh axis runs over, the one named last changes fastest.
Arguments:
- queries: bfloat16 [16384, 2048], P(('dates', 'ctx')), parts along dimension 0, may hold values from -6 to 6
- key_projection_rows: bfloat16 [16384, 1024], P(('dates', 'ctx')), parts along dimension 0, may hold values from -6 to 6
- value_projection_rows: bfloat16 [16384, 1024], P(('dates', 'ctx')), parts along dimension 0, may hold values from -6 to 6
- query_gain: float32 [256], replicated, may hold values from 0.5 to 1.5
- key_norm_gain: float32 [256], replicated, may hold values from 0.5 to 1.5
- session_flags: int32 [16384], P(('dates', 'ctx')), parts along dimension 0, may hold values from 0 to 1, as said below
- valid_length: int32 [2], P('dates'), parts along dimension 0, may hold values from 7936 to 8192
Outputs:
- attended: bfloat16 [16384, 2048], P(('dates', 'ctx')), parts along dimension 0
The draws below stay inside these ranges and needn't reach their ends.
There are 2 independent parts, one for each index of `dates`. The reference program is written for one: setup_inputs(seed, part) draws one part's arguments, and reference() takes and returns one part's arrays. A program takes and returns all parts, laid end to end along the dimension named above; an argument that names none is the same for every part. Nothing has to cross between parts.
Inputs may be any that keep to these rules, and one draw needn't show every extreme that they name: `session_flags`: a 1 marks the first tick of a session; tick 0 always begins one; the ticks of some devices hold no session start.
All inputs are finite; a program needn't handle non-finite values.
Results may differ from the reference program's by a relative error of at most 0.012.
Values may be sent and summed in bfloat16 or wider, within the bound.
A program may use at most 128 MiB of HBM per device.

```python
import jax
import jax.numpy as jnp
from jax import lax

QUERY_HEADS = 8
KEY_VALUE_HEADS = 4
HEAD_DIMENSION = 256
WINDOW_TICKS = 1024
TOK_DEV = 512
CONTEXT_TICKS = 8192


def draw_session_flags(key, part):
    positions = jnp.arange(CONTEXT_TICKS, dtype=jnp.int32)
    owners = positions // TOK_DEV
    within = positions % TOK_DEV
    phase = owners % 4
    random_marks = jax.random.randint(key, (CONTEXT_TICKS,), 0, 2 * TOK_DEV) == 0
    forced = ((phase == 0) | (phase == 3)) & (within == TOK_DEV - 1)
    cleared = (phase == 0) | (phase == 1)
    flags = jnp.where(cleared, False, random_marks) | forced | (positions == 0)
    return flags.astype(jnp.int32)


def steps_of(stream_key, dims, cuts, least, top_value):
    def one(dim, parts):
        heights = jax.random.uniform(jax.random.fold_in(jax.random.fold_in(stream_key, 6), dim), (parts,), jnp.float32, least / len(cuts), top_value / len(cuts))
        return jnp.repeat(jnp.exp(heights), dims[dim] // parts).reshape((-1,) + (1,) * (len(dims) - dim - 1))

    loudness = one(*cuts[0])
    for cut in cuts[1:]:
        loudness = loudness * one(*cut)
    return loudness


def bell_draw(rng, shape, scale, bound, pieces=(), held_as=jnp.bfloat16):
    level = steps_of(rng, shape, pieces, -0.22, 0.18) if pieces else 1.0
    drawn = jax.random.normal(rng, shape, jnp.float32) * scale * level
    return jnp.minimum(jnp.maximum(drawn, -bound), bound).astype(held_as)


def setup_inputs(seed: int = 0, part: int = 0) -> dict:
    key_of = jax.random.split(jax.random.key(seed), 8)
    own_keys = jax.random.split(jax.random.fold_in(key_of[7], part), 8)
    queries = bell_draw(own_keys[0], (CONTEXT_TICKS, QUERY_HEADS * HEAD_DIMENSION), 1.0, 6.0, ((0, 16),))
    key_projection_rows = bell_draw(own_keys[1], (CONTEXT_TICKS, KEY_VALUE_HEADS * HEAD_DIMENSION), 1.0, 6.0, ((0, 16),))
    value_projection_rows = bell_draw(own_keys[2], (CONTEXT_TICKS, KEY_VALUE_HEADS * HEAD_DIMENSION), 1.0, 6.0, ((0, 16),))
    query_gain = jnp.clip(1.0 + 0.1 * jax.random.normal(key_of[3], (HEAD_DIMENSION,), jnp.float32), 0.5, 1.5)
    key_norm_gain = jnp.clip(1.0 + 0.1 * jax.random.normal(key_of[4], (HEAD_DIMENSION,), jnp.float32), 0.5, 1.5)
    session_flags = draw_session_flags(jax.random.fold_in(jax.random.fold_in(key_of[7], part), 71), part)
    valid_length = jax.random.randint(own_keys[6], (1,), CONTEXT_TICKS - TOK_DEV // 2, CONTEXT_TICKS + 1).astype(jnp.int32)
    return dict(queries=queries, key_projection_rows=key_projection_rows, value_projection_rows=value_projection_rows, query_gain=query_gain, key_norm_gain=key_norm_gain, session_flags=session_flags, valid_length=valid_length)


def rootmean_rotary(inputs, gain, tick_positions, heads):
    grand_total = inputs.shape[0]
    vectors = inputs.astype(jnp.float32).reshape(grand_total, heads, HEAD_DIMENSION)
    vectors = vectors * lax.rsqrt(lax.optimization_barrier(jnp.mean(vectors * vectors, axis=-1, keepdims=True)) + 1e-06) * gain.astype(jnp.float32)
    half_width = HEAD_DIMENSION // 2
    inverse = 10000.0 ** (-(jnp.arange(half_width, dtype=jnp.float32) * (2.0 / HEAD_DIMENSION)))
    angles = tick_positions.astype(jnp.float32)[:, None, None] * inverse
    cosine = jnp.cos(angles)
    sine = jnp.sin(angles)
    first = vectors[..., :half_width]
    second = vectors[..., half_width:]
    return jnp.concatenate([first * cosine - second * sine, second * cosine + first * sine], axis=-1).astype(jnp.bfloat16)

def attend(query_tile_block, key_tile_block, value_tile_block, query_pos, key_pos, starts, limit):
    block_extent = query_tile_block.shape[0]
    grouped_heads = query_tile_block.reshape(block_extent, KEY_VALUE_HEADS, QUERY_HEADS // KEY_VALUE_HEADS, HEAD_DIMENSION).astype(jnp.float32)
    scores = jnp.einsum('qhgd,khd->hgqk', grouped_heads, key_tile_block.astype(jnp.float32)) * HEAD_DIMENSION ** (-0.5)
    allowed = (key_pos[None, :] <= query_pos[:, None]) & (key_pos[None, :] > query_pos[:, None] - WINDOW_TICKS) & (key_pos[None, :] >= starts[:, None])
    weights = jnp.where(allowed, jnp.exp(scores), jnp.float32(0.0))
    totals = lax.optimization_barrier(jnp.sum(weights, axis=-1))
    rounded = lax.optimization_barrier(weights.astype(jnp.bfloat16)).astype(jnp.float32)
    mixed = jnp.einsum('hgqk,khd->qhgd', rounded, value_tile_block.astype(jnp.float32))
    mixed = mixed / jnp.transpose(totals, (2, 0, 1))[..., None]
    mixed = mixed.reshape(block_extent, QUERY_HEADS * HEAD_DIMENSION)
    mixed = jnp.where((query_pos < limit)[:, None], mixed, jnp.float32(0.0))
    return mixed.astype(jnp.bfloat16)

def reference(queries, key_projection_rows, value_projection_rows, query_gain, key_norm_gain, session_flags, valid_length):
    grand_total = queries.shape[0]
    tick_positions = jnp.arange(grand_total, dtype=jnp.int32)
    normed_q = rootmean_rotary(queries, query_gain, tick_positions, QUERY_HEADS)
    normalized_keys = rootmean_rotary(key_projection_rows, key_norm_gain, tick_positions, KEY_VALUE_HEADS)
    value_tensor3 = value_projection_rows.reshape(grand_total, KEY_VALUE_HEADS, HEAD_DIMENSION)
    padded_key_rows = jnp.concatenate([jnp.zeros((WINDOW_TICKS, KEY_VALUE_HEADS, HEAD_DIMENSION), jnp.bfloat16), normalized_keys], axis=0)
    padded_value_rows = jnp.concatenate([jnp.zeros((WINDOW_TICKS, KEY_VALUE_HEADS, HEAD_DIMENSION), jnp.bfloat16), value_tensor3], axis=0)
    starts = lax.cummax(jnp.where(session_flags == 1, tick_positions, 0).astype(jnp.int32), axis=0)
    limit = valid_length[0]

    def one_block(block_index):
        first_row = (block_index * TOK_DEV).astype(jnp.int32)
        query_tile_block = lax.dynamic_slice_in_dim(normed_q, first_row, TOK_DEV, 0)
        key_tile_block = lax.dynamic_slice_in_dim(padded_key_rows, first_row, WINDOW_TICKS + TOK_DEV, 0)
        value_tile_block = lax.dynamic_slice_in_dim(padded_value_rows, first_row, WINDOW_TICKS + TOK_DEV, 0)
        start_block = lax.dynamic_slice_in_dim(starts, first_row, TOK_DEV, 0)
        query_pos = first_row + jnp.arange(TOK_DEV, dtype=jnp.int32)
        key_pos = first_row - WINDOW_TICKS + jnp.arange(WINDOW_TICKS + TOK_DEV, dtype=jnp.int32)
        return attend(query_tile_block, key_tile_block, value_tile_block, query_pos, key_pos, start_block, limit)
    blocks = lax.map(one_block, jnp.arange(grand_total // TOK_DEV, dtype=jnp.int32))
    return blocks.reshape(grand_total, QUERY_HEADS * HEAD_DIMENSION)
```

```python
import functools

import jax
import jax.numpy as jnp
import numpy as np
from jax import lax
from jax.experimental import pallas as pl
from jax.experimental.pallas import tpu as pltpu
from jax.sharding import PartitionSpec as P

QUERY_HEADS = 8
KEY_VALUE_HEADS = 4
HEAD = 256
HALF = HEAD // 2
WINDOW = 1024
ROWS = 512
SUB = 256
MESH = pl.DeviceIdType.MESH


def kernel(
    count,
    q_hbm,
    k_hbm,
    v_hbm,
    gains_ref,
    flags_ref,
    limit_ref,
    rope_hbm,
    inverse_ref,
    o_hbm,
    q_in,
    k_in,
    rope,
    kbuf,
    vbuf,
    ksend,
    qbuf,
    qsend,
    flags,
    low,
    acc,
    total,
    stage,
    load_sem,
    vloc_sem,
    fsend_sem,
    frecv_sem,
    pk_send,
    pk_recv,
    pv_send,
    pv_recv,
    k_send,
    k_recv,
    v_send,
    v_recv,
    q_send,
    q_recv,
    o_loc,
    o_send,
    o_recv,
):
    me = lax.axis_index("ctx")
    core = lax.rem(me, 2)
    other = 1 - core
    chip = me // 2
    chips = count // 2
    after = lax.rem(chip + 1, chips)
    before = lax.rem(chip + chips - 1, chips)
    partner = chip * 2 + other

    def span(index, width):
        return pl.ds(pl.multiple_of(index * width, width), width)

    def remote(src, dst, send, recv, target):
        return pltpu.make_async_remote_copy(
            src_ref=src,
            dst_ref=dst,
            send_sem=send,
            recv_sem=recv,
            device_id={"ctx": target},
            device_id_type=MESH,
        )

    load_k = pltpu.make_async_copy(k_hbm, k_in, load_sem.at[0])
    load_r = pltpu.make_async_copy(rope_hbm, rope, load_sem.at[1])
    load_q = pltpu.make_async_copy(q_hbm, q_in, load_sem.at[2])
    load_k.start()
    load_r.start()
    load_q.start()
    own_rows = span(2 + core, ROWS)
    v_local = [
        pltpu.make_async_copy(
            v_hbm.at[:, span(core * 2 + h, HEAD)], vbuf.at[h, own_rows], vloc_sem.at[h]
        )
        for h in range(2)
    ]
    for copy in v_local:
        copy.start()
    flags[2 + core] = jnp.broadcast_to(flags_ref[...], (8, ROWS))

    barrier = pltpu.get_barrier_semaphore()
    for target in (before * 2, before * 2 + 1, after * 2, after * 2 + 1, partner):
        pl.semaphore_signal(barrier, inc=1, device_id={"ctx": target}, device_id_type=MESH)
    pl.semaphore_wait(barrier, 5)

    near, far = after * 2 + core, after * 2 + other
    flag_out = [
        remote(flags.at[2 + core], flags.at[2 + core], fsend_sem.at[0], frecv_sem.at[2], partner),
        remote(flags.at[2 + core], flags.at[core], fsend_sem.at[1], frecv_sem.at[core], near),
        remote(flags.at[2 + core], flags.at[core], fsend_sem.at[2], frecv_sem.at[core], far),
    ]
    for copy in flag_out:
        copy.start()

    there = span(core, ROWS)
    v_out = []
    for h in range(2):
        mine = v_hbm.at[:, span(core * 2 + h, HEAD)]
        theirs = v_hbm.at[:, span(other * 2 + h, HEAD)]
        v_out += [
            remote(mine, vbuf.at[h, there], v_send.at[h, 0], v_recv.at[h, core], near),
            remote(theirs, vbuf.at[h, there], v_send.at[h, 1], v_recv.at[h, core], far),
        ]
    for copy in v_out:
        copy.start()
    pv_out = [
        remote(
            v_hbm.at[:, span(other * 2 + h, HEAD)],
            vbuf.at[h, own_rows],
            pv_send.at[h],
            pv_recv.at[h],
            partner,
        )
        for h in range(2)
    ]

    device_start = me * ROWS
    base = device_start.astype(jnp.float32) * inverse_ref[...]
    base_cos, base_sin = jnp.cos(base)[:1], jnp.sin(base)[:1]
    load_r.wait()
    row_cos, row_sin = rope[0], rope[1]
    rope[0] = base_cos * row_cos - base_sin * row_sin
    rope[1] = base_sin * row_cos + base_cos * row_sin

    def normed(raw, gain, scale):
        x = raw.astype(jnp.float32)
        mean = jnp.sum(x * x, axis=-1, keepdims=True) * (1.0 / HEAD)
        x = x * lax.rsqrt(mean + 1e-06) * gain
        a, b = x[:, :HALF], x[:, HALF:]
        cosine, sine = rope[0], rope[1]
        first = (a * cosine - b * sine).astype(jnp.bfloat16)
        second = (b * cosine + a * sine).astype(jnp.bfloat16)
        if scale != 1.0:
            first, second = first * jnp.bfloat16(scale), second * jnp.bfloat16(scale)
        return first, second

    load_k.wait()
    k_out, pk_out = [], []
    for h in range(2):
        first, second = normed(k_in[:, span(core * 2 + h, HEAD)], gains_ref[1:2], 1.0)
        kbuf[h, own_rows, :HALF] = first
        kbuf[h, own_rows, HALF:] = second
        first, second = normed(k_in[:, span(other * 2 + h, HEAD)], gains_ref[1:2], 1.0)
        ksend[h, :, :HALF] = first
        ksend[h, :, HALF:] = second
        pair = [
            remote(kbuf.at[h, own_rows], kbuf.at[h, there], k_send.at[h, 0], k_recv.at[h, core], near),
            remote(ksend.at[h], kbuf.at[h, there], k_send.at[h, 1], k_recv.at[h, core], far),
        ]
        for copy in pair:
            copy.start()
        k_out += pair
        pk_out.append(
            remote(ksend.at[h], kbuf.at[h, own_rows], pk_send.at[h], pk_recv.at[h], partner)
        )
        pk_out[-1].start()
        pv_out[h].start()

    load_q.wait()
    mine_rows = span(core, ROWS)
    q_out = []
    for j in range(4):
        first, second = normed(q_in[:, span(other * 4 + j, HEAD)], gains_ref[0:1], HEAD**-0.5)
        qsend[j, :, :HALF] = first
        qsend[j, :, HALF:] = second
        q_out.append(
            remote(qsend.at[j], qbuf.at[j // 2, j % 2, mine_rows], q_send.at[j], q_recv.at[j], partner)
        )
        q_out[-1].start()
    for j in range(4):
        first, second = normed(q_in[:, span(core * 4 + j, HEAD)], gains_ref[0:1], HEAD**-0.5)
        qbuf[j // 2, j % 2, mine_rows, :HALF] = first
        qbuf[j // 2, j % 2, mine_rows, HALF:] = second

    remote(flags.at[0], flags.at[2 + other], fsend_sem.at[0], frecv_sem.at[2], partner).wait_recv()
    for s in range(2):
        remote(flags.at[0], flags.at[s], fsend_sem.at[0], frecv_sem.at[s], partner).wait_recv()
    first_tick = (chip * 2 - 2) * ROWS
    column = lax.broadcasted_iota(jnp.int32, (8, ROWS), 1)

    def marks(slot):
        place = column + slot * ROWS
        return jnp.where((flags[slot] == 1) & (place + first_tick >= 0), place, -first_tick)

    behind = jnp.max(jnp.maximum(marks(0), marks(1)), axis=1, keepdims=True)[:1]
    row = lax.broadcasted_iota(jnp.int32, (ROWS, ROWS), 0)
    col = lax.broadcasted_iota(jnp.int32, (ROWS, ROWS), 1)
    for b in range(2):
        line = marks(2 + b)[:1]
        seen = jnp.where(col <= row, jnp.broadcast_to(line, (ROWS, ROWS)), -first_tick)
        start = jnp.maximum(jnp.max(seen, axis=1, keepdims=True), behind)
        behind = jnp.maximum(behind, jnp.max(line, axis=1, keepdims=True))
        tick = lax.broadcasted_iota(jnp.int32, (ROWS, 1), 0) + (2 + b) * ROWS
        start = jnp.maximum(start, tick - (WINDOW - 1))
        low[pl.ds(b * ROWS, ROWS)] = jnp.broadcast_to(start, (ROWS, 128))

    def part(h, u, key_first, keys, first_use):
        ticks = pl.ds(u * SUB, SUB)
        q = qbuf[h, :, ticks, :].reshape(2 * SUB, HEAD)
        k = kbuf[h, pl.ds(key_first, keys), :]
        v = vbuf[h, pl.ds(key_first, keys), :]
        score = lax.dot_general(q, k, (((1,), (1,)), ((), ())), preferred_element_type=jnp.float32)
        place = lax.broadcasted_iota(jnp.int32, (SUB, keys), 1) + key_first
        allowed = place >= low[ticks][:, :1]
        if key_first + keys > WINDOW + u * SUB:
            tick = lax.broadcasted_iota(jnp.int32, (SUB, keys), 0) + (WINDOW + u * SUB)
            allowed = allowed & (place <= tick)
        weight = jnp.where(allowed[None], jnp.exp(score).reshape(2, SUB, keys), 0.0)
        weight = weight.reshape(2 * SUB, keys)
        lanes = weight[:, :128]
        for i in range(1, keys // 128):
            lanes = lanes + weight[:, i * 128 : (i + 1) * 128]
        mixed = jnp.dot(weight.astype(jnp.bfloat16), v, preferred_element_type=jnp.float32)
        if first_use:
            acc[h, u] = mixed
            total[h, u] = lanes
        else:
            acc[h, u] += mixed
            total[h, u] += lanes

    for copy in v_local:
        copy.wait()
    for j in range(4):
        remote(qsend.at[j], qbuf.at[j // 2, j % 2, span(other, ROWS)], q_send.at[j], q_recv.at[j], partner).wait_recv()

    partner_rows = span(2 + other, ROWS)

    def own(h, carry):
        remote(ksend.at[0], kbuf.at[h, partner_rows], pk_send.at[0], pk_recv.at[h], partner).wait_recv()
        remote(ksend.at[0], vbuf.at[h, partner_rows], pv_send.at[0], pv_recv.at[h], partner).wait_recv()
        part(h, 0, WINDOW, 256, True)
        part(h, 1, WINDOW, 512, True)
        part(h, 2, WINDOW, 512, True)
        part(h, 2, WINDOW + 512, 256, False)
        part(h, 3, WINDOW, 512, True)
        part(h, 3, WINDOW + 512, 512, False)
        return carry

    lax.fori_loop(0, 2, own, 0)

    limit = limit_ref[0]

    def finish(h, u):
        whole = jnp.sum(total[h, u], axis=-1, keepdims=True)
        value = (acc[h, u] / whole).reshape(2, SUB, HEAD)
        tick = lax.broadcasted_iota(jnp.int32, (SUB, HEAD), 0) + (first_tick + WINDOW + u * SUB)
        value = jnp.where((tick < limit)[None], value, 0.0).astype(jnp.bfloat16)
        stage[h, :, pl.ds(u * SUB, SUB), :] = value

    def out_copies(h, j):
        columns = span(core * 4 + h * 2 + j, HEAD)
        local = pltpu.make_async_copy(
            stage.at[h, j, mine_rows], o_hbm.at[:, columns], o_loc.at[h, j]
        )
        away = remote(
            stage.at[h, j, span(other, ROWS)],
            o_hbm.at[:, columns],
            o_send.at[h, j],
            o_recv.at[h, j],
            partner,
        )
        return local, away

    def far_keys(h, carry):
        for s in range(2):
            rows = pl.ds(s * ROWS, ROWS)
            remote(ksend.at[0], vbuf.at[h, rows], v_send.at[0, 0], v_recv.at[h, s], partner).wait_recv()
            remote(ksend.at[0], kbuf.at[h, rows], k_send.at[0, 0], k_recv.at[h, s], partner).wait_recv()
            if s == 0:
                part(h, 0, 0, 512, False)
                part(h, 1, 256, 256, False)
            else:
                part(h, 0, 512, 512, False)
                part(h, 1, 512, 512, False)
                part(h, 2, 512, 512, False)
                part(h, 3, 768, 256, False)
        for u in range(4):
            finish(h, u)
        for j in range(2):
            for copy in out_copies(h, j):
                copy.start()
        return carry

    lax.fori_loop(0, 2, far_keys, 0)

    for h in range(2):
        for j in range(2):
            local, away = out_copies(h, j)
            local.wait()
            away.wait_send()
            columns = span(other * 4 + h * 2 + j, HEAD)
            remote(stage.at[h, j, mine_rows], o_hbm.at[:, columns], o_send.at[h, j], o_recv.at[h, j], partner).wait_recv()
    for copy in flag_out + v_out + pv_out + k_out + pk_out + q_out:
        copy.wait_send()


def solution(mesh):
    count = mesh.shape["ctx"]
    inverse = 10000.0 ** (-(np.arange(HALF, dtype=np.float64) * (2.0 / HEAD)))
    angle = np.arange(ROWS, dtype=np.float64)[:, None] * inverse
    table = np.stack([np.cos(angle), np.sin(angle)]).astype(np.float32)

    def body(queries, keys, values, query_gain, key_gain, session_flags, valid_length):
        assert queries.shape[0] == ROWS and 2 * ROWS == WINDOW
        gains = jnp.stack([query_gain, key_gain])
        bf16, f32, i32 = jnp.bfloat16, jnp.float32, jnp.int32
        dma = pltpu.SemaphoreType.DMA
        anywhere = pl.BlockSpec(memory_space=pl.ANY)
        vmem = pl.BlockSpec(memory_space=pltpu.VMEM)
        smem = pl.BlockSpec(memory_space=pltpu.SMEM)
        return pl.pallas_call(
            functools.partial(kernel, count),
            out_shape=jax.ShapeDtypeStruct((ROWS, QUERY_HEADS * HEAD), bf16),
            in_specs=[anywhere, anywhere, anywhere, vmem, vmem, smem, anywhere, vmem],
            out_specs=anywhere,
            scratch_shapes=[
                pltpu.VMEM((ROWS, QUERY_HEADS * HEAD), bf16),
                pltpu.VMEM((ROWS, KEY_VALUE_HEADS * HEAD), bf16),
                pltpu.VMEM((2, ROWS, HALF), f32),
                pltpu.VMEM((2, 4 * ROWS, HEAD), bf16),
                pltpu.VMEM((2, 4 * ROWS, HEAD), bf16),
                pltpu.VMEM((2, ROWS, HEAD), bf16),
                pltpu.VMEM((2, 2, 2 * ROWS, HEAD), bf16),
                pltpu.VMEM((4, ROWS, HEAD), bf16),
                pltpu.VMEM((4, 8, ROWS), i32),
                pltpu.VMEM((2 * ROWS, 128), i32),
                pltpu.VMEM((2, 4, 2 * SUB, HEAD), f32),
                pltpu.VMEM((2, 4, 2 * SUB, 128), f32),
                pltpu.VMEM((2, 2, 2 * ROWS, HEAD), bf16),
                dma((3,)),
                dma((2,)),
                dma((3,)),
                dma((3,)),
                dma((2,)),
                dma((2,)),
                dma((2,)),
                dma((2,)),
                dma((2, 2)),
                dma((2, 2)),
                dma((2, 2)),
                dma((2, 2)),
                dma((4,)),
                dma((4,)),
                dma((2, 2)),
                dma((2, 2)),
                dma((2, 2)),
            ],
            compiler_params=pltpu.CompilerParams(
                collective_id=0, has_side_effects=True, vmem_limit_bytes=48 << 20
            ),
        )(
            queries,
            keys,
            values,
            gains,
            session_flags.reshape(1, ROWS),
            valid_length,
            jnp.asarray(table),
            jnp.asarray(np.broadcast_to(inverse.astype(np.float32), (8, HALF))),
        )

    return jax.shard_map(
        body,
        mesh=mesh,
        in_specs=(
            P(("dates", "ctx"), None),
            P(("dates", "ctx"), None),
            P(("dates", "ctx"), None),
            P(),
            P(),
            P(("dates", "ctx")),
            P("dates"),
        ),
        out_specs=P(("dates", "ctx"), None),
        check_vma=False,
    )
```

```python
import functools

import jax
import jax.numpy as jnp
import numpy as np
from jax import lax
from jax.experimental import pallas as pl
from jax.experimental.pallas import tpu as pltpu
from jax.sharding import PartitionSpec as P

QUERY_HEADS = 8
KEY_VALUE_HEADS = 4
HEAD = 256
HALF = HEAD // 2
WINDOW = 1024
ROWS = 512
SUB = 256
MESH = pl.DeviceIdType.MESH


def kernel(
    count,
    q_hbm,
    k_hbm,
    v_hbm,
    q_gain,
    k_gain,
    flags_ref,
    rope_hbm,
    o_hbm,
    q_in,
    k_in,
    rope,
    kbuf,
    vbuf,
    ksend,
    qbuf,
    qsend,
    flags,
    low,
    acc,
    total,
    stage,
    held,
    load_sem,
    vloc_sem,
    fsend_sem,
    frecv_sem,
    pk_send,
    pk_recv,
    pv_send,
    pv_recv,
    k_send,
    k_recv,
    v_send,
    v_recv,
    q_send,
    q_recv,
    o_loc,
    o_send,
    o_recv,
):
    me = lax.axis_index("ctx")
    core = lax.rem(me, 2)
    other = 1 - core
    chip = me // 2
    chips = count // 2
    after = lax.rem(chip + 1, chips)
    before = lax.rem(chip + chips - 1, chips)
    partner = chip * 2 + other

    def span(index, width):
        return pl.ds(pl.multiple_of(index * width, width), width)

    def remote(src, dst, send, recv, target):
        return pltpu.make_async_remote_copy(
            src_ref=src,
            dst_ref=dst,
            send_sem=send,
            recv_sem=recv,
            device_id={"ctx": target},
            device_id_type=MESH,
        )

    load_k = pltpu.make_async_copy(k_hbm, k_in, load_sem.at[0])
    load_r = pltpu.make_async_copy(rope_hbm, rope, load_sem.at[1])
    load_q = pltpu.make_async_copy(q_hbm, q_in, load_sem.at[2])
    load_k.start()
    load_r.start()
    load_q.start()
    own_rows = span(2 + core, ROWS)
    v_local = [
        pltpu.make_async_copy(
            v_hbm.at[:, span(core * 2 + h, HEAD)], vbuf.at[h, own_rows], vloc_sem.at[h]
        )
        for h in range(2)
    ]
    for copy in v_local:
        copy.start()
    flags[2 + core] = jnp.broadcast_to(flags_ref[...], (8, ROWS))

    barrier = pltpu.get_barrier_semaphore()
    for target in (before * 2, before * 2 + 1, after * 2, after * 2 + 1, partner):
        pl.semaphore_signal(barrier, inc=1, device_id={"ctx": target}, device_id_type=MESH)
    pl.semaphore_wait(barrier, 5)

    near, far = after * 2 + core, after * 2 + other
    flag_out = [
        remote(flags.at[2 + core], flags.at[2 + core], fsend_sem.at[0], frecv_sem.at[2], partner),
        remote(flags.at[2 + core], flags.at[core], fsend_sem.at[1], frecv_sem.at[core], near),
        remote(flags.at[2 + core], flags.at[core], fsend_sem.at[2], frecv_sem.at[core], far),
    ]
    for copy in flag_out:
        copy.start()

    there = span(core, ROWS)
    v_out = []
    for h in range(2):
        mine = v_hbm.at[:, span(core * 2 + h, HEAD)]
        theirs = v_hbm.at[:, span(other * 2 + h, HEAD)]
        v_out += [
            remote(mine, vbuf.at[h, there], v_send.at[h, 0], v_recv.at[h, core], near),
            remote(theirs, vbuf.at[h, there], v_send.at[h, 1], v_recv.at[h, core], far),
        ]
    for copy in v_out[:2]:
        copy.start()
    pv_out = [
        remote(
            v_hbm.at[:, span(other * 2 + h, HEAD)],
            vbuf.at[h, own_rows],
            pv_send.at[h],
            pv_recv.at[h],
            partner,
        )
        for h in range(2)
    ]

    device_start = me * ROWS
    load_r.wait()
    base = device_start.astype(jnp.float32) * rope[2, :8]
    base_cos, base_sin = jnp.cos(base)[:1], jnp.sin(base)[:1]
    row_cos, row_sin = rope[0], rope[1]
    rope[0] = base_cos * row_cos - base_sin * row_sin
    rope[1] = base_sin * row_cos + base_cos * row_sin

    def normed(raw, gain, scale):
        x = raw.astype(jnp.float32)
        mean = jnp.sum(x * x, axis=-1, keepdims=True) * (1.0 / HEAD)
        x = x * lax.rsqrt(mean + 1e-06) * gain
        a, b = x[:, :HALF], x[:, HALF:]
        cosine, sine = rope[0], rope[1]
        first = (a * cosine - b * sine).astype(jnp.bfloat16)
        second = (b * cosine + a * sine).astype(jnp.bfloat16)
        if scale != 1.0:
            first, second = first * jnp.bfloat16(scale), second * jnp.bfloat16(scale)
        return first, second

    load_k.wait()
    k_out, pk_out = [], []
    for h in range(2):
        first, second = normed(k_in[:, span(core * 2 + h, HEAD)], k_gain[...], 1.0)
        kbuf[h, own_rows, :HALF] = first
        kbuf[h, own_rows, HALF:] = second
        first, second = normed(k_in[:, span(other * 2 + h, HEAD)], k_gain[...], 1.0)
        ksend[h, :, :HALF] = first
        ksend[h, :, HALF:] = second
        pair = [
            remote(kbuf.at[h, own_rows], kbuf.at[h, there], k_send.at[h, 0], k_recv.at[h, core], near),
            remote(ksend.at[h], kbuf.at[h, there], k_send.at[h, 1], k_recv.at[h, core], far),
        ]
        for copy in pair:
            copy.start()
        k_out += pair
        pk_out.append(
            remote(ksend.at[h], kbuf.at[h, own_rows], pk_send.at[h], pk_recv.at[h], partner)
        )
        if h == 1:
            for copy in v_out[2:]:
                copy.start()
        pk_out[-1].start()
        pv_out[h].start()

    load_q.wait()
    mine_rows = span(core, ROWS)
    q_out = []
    for j in range(4):
        first, second = normed(q_in[:, span(other * 4 + j, HEAD)], q_gain[...], HEAD**-0.5)
        qsend[j, :, :HALF] = first
        qsend[j, :, HALF:] = second
        q_out.append(
            remote(qsend.at[j], qbuf.at[j // 2, j % 2, mine_rows], q_send.at[j], q_recv.at[j], partner)
        )
        q_out[-1].start()
    for j in range(4):
        first, second = normed(q_in[:, span(core * 4 + j, HEAD)], q_gain[...], HEAD**-0.5)
        qbuf[j // 2, j % 2, mine_rows, :HALF] = first
        qbuf[j // 2, j % 2, mine_rows, HALF:] = second

    remote(flags.at[0], flags.at[2 + other], fsend_sem.at[0], frecv_sem.at[2], partner).wait_recv()
    for s in range(2):
        remote(flags.at[0], flags.at[s], fsend_sem.at[0], frecv_sem.at[s], partner).wait_recv()
    first_tick = (chip * 2 - 2) * ROWS
    column = lax.broadcasted_iota(jnp.int32, (8, ROWS), 1)

    def marks(slot):
        place = column + slot * ROWS
        return jnp.where((flags[slot] == 1) & (place + first_tick >= 0), place, -first_tick)

    behind = jnp.max(jnp.maximum(marks(0), marks(1)), axis=1, keepdims=True)[:1]
    row = lax.broadcasted_iota(jnp.int32, (ROWS, ROWS), 0)
    col = lax.broadcasted_iota(jnp.int32, (ROWS, ROWS), 1)
    for b in range(2):
        line = marks(2 + b)[:1]
        seen = jnp.where(col <= row, jnp.broadcast_to(line, (ROWS, ROWS)), -first_tick)
        start = jnp.maximum(jnp.max(seen, axis=1, keepdims=True), behind)
        behind = jnp.maximum(behind, jnp.max(line, axis=1, keepdims=True))
        tick = lax.broadcasted_iota(jnp.int32, (ROWS, 1), 0) + (2 + b) * ROWS
        start = jnp.maximum(start, tick - (WINDOW - 1))
        low[pl.ds(b * ROWS, ROWS)] = jnp.broadcast_to(start, (ROWS, 128))

    def weigh(h, u, key_first, keys):
        ticks = pl.ds(u * SUB, SUB)
        q = qbuf[h, :, ticks, :].reshape(2 * SUB, HEAD)
        k = kbuf[h, pl.ds(key_first, keys), :]
        score = lax.dot_general(q, k, (((1,), (1,)), ((), ())), preferred_element_type=jnp.float32)
        place = lax.broadcasted_iota(jnp.int32, (SUB, keys), 1) + key_first
        allowed = place >= low[ticks][:, :1]
        if key_first + keys > WINDOW + u * SUB:
            tick = lax.broadcasted_iota(jnp.int32, (SUB, keys), 0) + (WINDOW + u * SUB)
            allowed = allowed & (place <= tick)
        weight = jnp.where(allowed[None], jnp.exp(score).reshape(2, SUB, keys), 0.0)
        weight = weight.reshape(2 * SUB, keys)
        lanes = weight[:, :128]
        for i in range(1, keys // 128):
            lanes = lanes + weight[:, i * 128 : (i + 1) * 128]
        return weight.astype(jnp.bfloat16), lanes

    def part(h, u, key_first, keys, first_use):
        weight, lanes = weigh(h, u, key_first, keys)
        v = vbuf[h, pl.ds(key_first, keys), :]
        mixed = jnp.dot(weight, v, preferred_element_type=jnp.float32)
        if first_use:
            acc[h, u] = mixed
            total[h, u] = lanes
        else:
            acc[h, u] += mixed
            total[h, u] += lanes

    for copy in v_local:
        copy.wait()
    for j in range(4):
        remote(qsend.at[j], qbuf.at[j // 2, j % 2, span(other, ROWS)], q_send.at[j], q_recv.at[j], partner).wait_recv()

    partner_rows = span(2 + other, ROWS)

    def own(h, carry):
        remote(ksend.at[0], kbuf.at[h, partner_rows], pk_send.at[0], pk_recv.at[h], partner).wait_recv()
        remote(ksend.at[0], vbuf.at[h, partner_rows], pv_send.at[0], pv_recv.at[h], partner).wait_recv()
        part(h, 0, WINDOW, 256, True)
        part(h, 1, WINDOW, 512, True)
        part(h, 2, WINDOW, 512, True)
        part(h, 2, WINDOW + 512, 256, False)
        part(h, 3, WINDOW, 512, True)
        part(h, 3, WINDOW + 512, 512, False)
        return carry

    lax.fori_loop(0, 2, own, 0)

    def finish(h, u):
        whole = jnp.sum(total[h, u], axis=-1, keepdims=True)
        value = (acc[h, u] / whole).reshape(2, SUB, HEAD)
        stage[h, :, pl.ds(u * SUB, SUB), :] = value.astype(jnp.bfloat16)

    def out_copies(h, j):
        columns = span(core * 4 + h * 2 + j, HEAD)
        local = pltpu.make_async_copy(
            stage.at[h, j, mine_rows], o_hbm.at[:, columns], o_loc.at[h, j]
        )
        away = remote(
            stage.at[h, j, span(other, ROWS)],
            o_hbm.at[:, columns],
            o_send.at[h, j],
            o_recv.at[h, j],
            partner,
        )
        return local, away

    def arrived(buffer, h, s, sems):
        remote(ksend.at[0], buffer.at[h, pl.ds(s * ROWS, ROWS)], k_send.at[0, 0], sems.at[h, s], partner).wait_recv()

    for s in range(2):
        arrived(vbuf, 0, s, v_recv)
        arrived(kbuf, 0, s, k_recv)
        if s == 0:
            part(0, 0, 0, 512, False)
            part(0, 1, 256, 256, False)
        else:
            for u in range(4):
                part(0, u, max(512, u * SUB), WINDOW - max(512, u * SUB), False)
    for u in range(4):
        finish(0, u)
    for j in range(2):
        for copy in out_copies(0, j):
            copy.start()

    for s in range(2):
        arrived(kbuf, 1, s, k_recv)
        for u in range(4):
            first, last = max(s * ROWS, u * SUB), (s + 1) * ROWS
            if first < last:
                weight, lanes = weigh(1, u, first, last - first)
                held[u, :, pl.ds(first, last - first)] = weight
                total[1, u] += lanes
    for s in range(2):
        arrived(vbuf, 1, s, v_recv)

    def mix(block):
        for u in (2 * block, 2 * block + 1):
            keys = pl.ds(u * SUB, WINDOW - u * SUB)
            acc[1, u] += jnp.dot(held[u, :, keys], vbuf[1, keys, :], preferred_element_type=jnp.float32)
            finish(1, u)

    def last_tiles(first_block):
        mix(first_block)
        for j in range(2):
            out_copies(1, j)[1].start()
        mix(1 - first_block)

    pl.when(core == 0)(lambda: last_tiles(1))
    pl.when(core == 1)(lambda: last_tiles(0))
    for j in range(2):
        out_copies(1, j)[0].start()

    for h in range(2):
        for j in range(2):
            local, away = out_copies(h, j)
            local.wait()
            away.wait_send()
            columns = span(other * 4 + h * 2 + j, HEAD)
            remote(stage.at[h, j, mine_rows], o_hbm.at[:, columns], o_send.at[h, j], o_recv.at[h, j], partner).wait_recv()
    for copy in flag_out + v_out + pv_out + k_out + pk_out + q_out:
        copy.wait_send()


def solution(mesh):
    count = mesh.shape["ctx"]
    inverse = 10000.0 ** (-(np.arange(HALF, dtype=np.float64) * (2.0 / HEAD)))
    angle = np.arange(ROWS, dtype=np.float64)[:, None] * inverse
    table = np.stack([np.cos(angle), np.sin(angle), 0 * angle + inverse]).astype(np.float32)

    def body(queries, keys, values, query_gain, key_gain, session_flags, valid_length):
        assert queries.shape[0] == ROWS and 2 * ROWS == WINDOW
        pinned = functools.partial(pltpu.with_memory_space_constraint, memory_space=pltpu.HBM)
        bf16, f32, i32 = jnp.bfloat16, jnp.float32, jnp.int32
        dma = pltpu.SemaphoreType.DMA
        anywhere = pl.BlockSpec(memory_space=pltpu.HBM)
        vmem = pl.BlockSpec(memory_space=pltpu.VMEM)
        mixed = pl.pallas_call(
            functools.partial(kernel, count),
            out_shape=pltpu.VMEM((ROWS, QUERY_HEADS * HEAD), bf16),
            in_specs=[anywhere, anywhere, anywhere, vmem, vmem, vmem, anywhere],
            out_specs=pl.BlockSpec(memory_space=pl.ANY),
            scratch_shapes=[
                pltpu.VMEM((ROWS, QUERY_HEADS * HEAD), bf16),
                pltpu.VMEM((ROWS, KEY_VALUE_HEADS * HEAD), bf16),
                pltpu.VMEM((3, ROWS, HALF), f32),
                pltpu.VMEM((2, 4 * ROWS, HEAD), bf16),
                pltpu.VMEM((2, 4 * ROWS, HEAD), bf16),
                pltpu.VMEM((2, ROWS, HEAD), bf16),
                pltpu.VMEM((2, 2, 2 * ROWS, HEAD), bf16),
                pltpu.VMEM((4, ROWS, HEAD), bf16),
                pltpu.VMEM((4, 8, ROWS), i32),
                pltpu.VMEM((2 * ROWS, 128), i32),
                pltpu.VMEM((2, 4, 2 * SUB, HEAD), f32),
                pltpu.VMEM((2, 4, 2 * SUB, 128), f32),
                pltpu.VMEM((2, 2, 2 * ROWS, HEAD), bf16),
                pltpu.VMEM((4, 2 * SUB, WINDOW), bf16),
                dma((3,)),
                dma((2,)),
                dma((3,)),
                dma((3,)),
                dma((2,)),
                dma((2,)),
                dma((2,)),
                dma((2,)),
                dma((2, 2)),
                dma((2, 2)),
                dma((2, 2)),
                dma((2, 2)),
                dma((4,)),
                dma((4,)),
                dma((2, 2)),
                dma((2, 2)),
                dma((2, 2)),
            ],
            compiler_params=pltpu.CompilerParams(
                collective_id=0, has_side_effects=True, vmem_limit_bytes=60 << 20
            ),
        )(
            pinned(queries),
            pinned(keys),
            pinned(values),
            query_gain.reshape(1, HEAD),
            key_gain.reshape(1, HEAD),
            session_flags.reshape(1, ROWS),
            pinned(jnp.asarray(table)),
        )
        tick = lax.axis_index("ctx") * ROWS + lax.broadcasted_iota(i32, mixed.shape, 0)
        return jnp.where(tick < valid_length[0], mixed, jnp.zeros((), bf16))

    return jax.shard_map(
        body,
        mesh=mesh,
        in_specs=(
            P(("dates", "ctx"), None),
            P(("dates", "ctx"), None),
            P(("dates", "ctx"), None),
            P(),
            P(),
            P(("dates", "ctx")),
            P("dates"),
        ),
        out_specs=P(("dates", "ctx"), None),
        check_vma=False,
    )
```

```python
import functools

import jax
import jax.numpy as jnp
import numpy as np
from jax import lax
from jax.experimental import pallas as pl
from jax.experimental.pallas import tpu as pltpu
from jax.sharding import PartitionSpec as P

QUERY_HEADS = 8
KEY_VALUE_HEADS = 4
HEAD = 256
HALF = HEAD // 2
WINDOW = 1024
ROWS = 512
SUB = 256
MESH = pl.DeviceIdType.MESH


def kernel(
    count,
    q_hbm,
    k_hbm,
    v_hbm,
    q_gain,
    k_gain,
    flags_ref,
    rope_hbm,
    o_hbm,
    q_in,
    k_in,
    rope,
    kbuf,
    vbuf,
    ksend,
    qbuf,
    qsend,
    flags,
    low,
    acc,
    total,
    stage,
    held,
    load_sem,
    vloc_sem,
    fsend_sem,
    frecv_sem,
    pk_send,
    pk_recv,
    pv_send,
    pv_recv,
    k_send,
    k_recv,
    v_send,
    v_recv,
    q_send,
    q_recv,
    o_loc,
    o_send,
    o_recv,
):
    me = lax.axis_index("ctx")
    core = lax.rem(me, 2)
    other = 1 - core
    chip = me // 2
    chips = count // 2
    after = lax.rem(chip + 1, chips)
    before = lax.rem(chip + chips - 1, chips)
    partner = chip * 2 + other
    has_after, has_before = chip < chips - 1, chip > 0

    def span(index, width):
        return pl.ds(pl.multiple_of(index * width, width), width)

    def remote(src, dst, send, recv, target):
        return pltpu.make_async_remote_copy(
            src_ref=src,
            dst_ref=dst,
            send_sem=send,
            recv_sem=recv,
            device_id={"ctx": target},
            device_id_type=MESH,
        )

    load_k = pltpu.make_async_copy(k_hbm, k_in, load_sem.at[0])
    load_r = pltpu.make_async_copy(rope_hbm, rope, load_sem.at[1])
    load_q = pltpu.make_async_copy(q_hbm, q_in, load_sem.at[2])
    load_k.start()
    load_r.start()
    load_q.start()
    own_rows = span(2 + core, ROWS)
    v_local = [
        pltpu.make_async_copy(
            v_hbm.at[:, span(core * 2 + h, HEAD)], vbuf.at[h, own_rows], vloc_sem.at[h]
        )
        for h in range(2)
    ]
    for copy in v_local:
        copy.start()
    flags[2 + core] = jnp.broadcast_to(flags_ref[...], (8, ROWS))

    barrier = pltpu.get_barrier_semaphore()

    def ready(target):
        pl.semaphore_signal(barrier, inc=1, device_id={"ctx": target}, device_id_type=MESH)

    @pl.when(has_before)
    def _():
        ready(before * 2)
        ready(before * 2 + 1)

    ready(partner)
    pl.when(has_after)(lambda: pl.semaphore_wait(barrier, 3))
    pl.when(jnp.logical_not(has_after))(lambda: pl.semaphore_wait(barrier, 1))

    def start_all(copies):
        @pl.when(has_after)
        def _():
            for copy in copies:
                copy.start()


    near, far = after * 2 + core, after * 2 + other
    flag_out = [
        remote(flags.at[2 + core], flags.at[2 + core], fsend_sem.at[0], frecv_sem.at[2], partner),
        remote(flags.at[2 + core], flags.at[core], fsend_sem.at[1], frecv_sem.at[core], near),
        remote(flags.at[2 + core], flags.at[core], fsend_sem.at[2], frecv_sem.at[core], far),
    ]
    flag_out[0].start()
    start_all(flag_out[1:])

    there = span(core, ROWS)
    v_out = []
    for h in range(2):
        mine = v_hbm.at[:, span(core * 2 + h, HEAD)]
        theirs = v_hbm.at[:, span(other * 2 + h, HEAD)]
        v_out += [
            remote(mine, vbuf.at[h, there], v_send.at[h, 0], v_recv.at[h, core], near),
            remote(theirs, vbuf.at[h, there], v_send.at[h, 1], v_recv.at[h, core], far),
        ]
    start_all(v_out[:2])
    pv_out = [
        remote(
            v_hbm.at[:, span(other * 2 + h, HEAD)],
            vbuf.at[h, own_rows],
            pv_send.at[h],
            pv_recv.at[h],
            partner,
        )
        for h in range(2)
    ]

    device_start = me * ROWS
    load_r.wait()
    base = device_start.astype(jnp.float32) * rope[2, :8]
    base_cos, base_sin = jnp.cos(base)[:1], jnp.sin(base)[:1]
    row_cos, row_sin = rope[0], rope[1]
    rope[0] = base_cos * row_cos - base_sin * row_sin
    rope[1] = base_sin * row_cos + base_cos * row_sin

    def normed(raw, gain, scale):
        x = raw.astype(jnp.float32)
        mean = jnp.sum(x * x, axis=-1, keepdims=True) * (1.0 / HEAD)
        x = x * lax.rsqrt(mean + 1e-06) * gain
        a, b = x[:, :HALF], x[:, HALF:]
        cosine, sine = rope[0], rope[1]
        first = (a * cosine - b * sine).astype(jnp.bfloat16)
        second = (b * cosine + a * sine).astype(jnp.bfloat16)
        if scale != 1.0:
            first, second = first * jnp.bfloat16(scale), second * jnp.bfloat16(scale)
        return first, second

    load_k.wait()
    k_out, pk_out = [], []
    for h in range(2):
        first, second = normed(k_in[:, span(core * 2 + h, HEAD)], k_gain[...], 1.0)
        kbuf[h, own_rows, :HALF] = first
        kbuf[h, own_rows, HALF:] = second
        first, second = normed(k_in[:, span(other * 2 + h, HEAD)], k_gain[...], 1.0)
        ksend[h, :, :HALF] = first
        ksend[h, :, HALF:] = second
        pair = [
            remote(kbuf.at[h, own_rows], kbuf.at[h, there], k_send.at[h, 0], k_recv.at[h, core], near),
            remote(ksend.at[h], kbuf.at[h, there], k_send.at[h, 1], k_recv.at[h, core], far),
        ]
        start_all(pair)
        k_out += pair
        pk_out.append(
            remote(ksend.at[h], kbuf.at[h, own_rows], pk_send.at[h], pk_recv.at[h], partner)
        )
        if h == 1:
            start_all(v_out[2:])
        pk_out[-1].start()
        pv_out[h].start()

    load_q.wait()
    mine_rows = span(core, ROWS)
    q_out = []
    for j in range(4):
        first, second = normed(q_in[:, span(other * 4 + j, HEAD)], q_gain[...], HEAD**-0.5)
        qsend[j, :, :HALF] = first
        qsend[j, :, HALF:] = second
        q_out.append(
            remote(qsend.at[j], qbuf.at[j // 2, j % 2, mine_rows], q_send.at[j], q_recv.at[j], partner)
        )
        q_out[-1].start()
    for j in range(4):
        first, second = normed(q_in[:, span(core * 4 + j, HEAD)], q_gain[...], HEAD**-0.5)
        qbuf[j // 2, j % 2, mine_rows, :HALF] = first
        qbuf[j // 2, j % 2, mine_rows, HALF:] = second

    remote(flags.at[0], flags.at[2 + other], fsend_sem.at[0], frecv_sem.at[2], partner).wait_recv()

    @pl.when(has_before)
    def _():
        for s in range(2):
            remote(flags.at[0], flags.at[s], fsend_sem.at[0], frecv_sem.at[s], partner).wait_recv()

    @pl.when(jnp.logical_not(has_before))
    def _():
        for s in range(2):
            flags[s] = jnp.zeros((8, ROWS), jnp.int32)

    first_tick = (chip * 2 - 2) * ROWS
    column = lax.broadcasted_iota(jnp.int32, (8, ROWS), 1)

    def marks(slot):
        place = column + slot * ROWS
        return jnp.where((flags[slot] == 1) & (place + first_tick >= 0), place, -first_tick)

    behind = jnp.max(jnp.maximum(marks(0), marks(1)), axis=1, keepdims=True)[:1]
    row = lax.broadcasted_iota(jnp.int32, (ROWS, ROWS), 0)
    col = lax.broadcasted_iota(jnp.int32, (ROWS, ROWS), 1)
    for b in range(2):
        line = marks(2 + b)[:1]
        seen = jnp.where(col <= row, jnp.broadcast_to(line, (ROWS, ROWS)), -first_tick)
        start = jnp.maximum(jnp.max(seen, axis=1, keepdims=True), behind)
        behind = jnp.maximum(behind, jnp.max(line, axis=1, keepdims=True))
        tick = lax.broadcasted_iota(jnp.int32, (ROWS, 1), 0) + (2 + b) * ROWS
        start = jnp.maximum(start, tick - (WINDOW - 1))
        low[pl.ds(b * ROWS, ROWS)] = jnp.broadcast_to(start, (ROWS, 128))

    def weigh(h, u, key_first, keys):
        ticks = pl.ds(u * SUB, SUB)
        q = qbuf[h, :, ticks, :].reshape(2 * SUB, HEAD)
        k = kbuf[h, pl.ds(key_first, keys), :]
        score = lax.dot_general(q, k, (((1,), (1,)), ((), ())), preferred_element_type=jnp.float32)
        place = lax.broadcasted_iota(jnp.int32, (SUB, keys), 1) + key_first
        allowed = place >= low[ticks][:, :1]
        if key_first + keys > WINDOW + u * SUB:
            tick = lax.broadcasted_iota(jnp.int32, (SUB, keys), 0) + (WINDOW + u * SUB)
            allowed = allowed & (place <= tick)
        weight = jnp.where(allowed[None], jnp.exp(score).reshape(2, SUB, keys), 0.0)
        weight = weight.reshape(2 * SUB, keys)
        lanes = weight[:, :128]
        for i in range(1, keys // 128):
            lanes = lanes + weight[:, i * 128 : (i + 1) * 128]
        return weight.astype(jnp.bfloat16), lanes

    def part(h, u, key_first, keys, first_use):
        weight, lanes = weigh(h, u, key_first, keys)
        v = vbuf[h, pl.ds(key_first, keys), :]
        mixed = jnp.dot(weight, v, preferred_element_type=jnp.float32)
        if first_use:
            acc[h, u] = mixed
            total[h, u] = lanes
        else:
            acc[h, u] += mixed
            total[h, u] += lanes

    for copy in v_local:
        copy.wait()
    for j in range(4):
        remote(qsend.at[j], qbuf.at[j // 2, j % 2, span(other, ROWS)], q_send.at[j], q_recv.at[j], partner).wait_recv()

    partner_rows = span(2 + other, ROWS)

    def own(h, carry):
        remote(ksend.at[0], kbuf.at[h, partner_rows], pk_send.at[0], pk_recv.at[h], partner).wait_recv()
        remote(ksend.at[0], vbuf.at[h, partner_rows], pv_send.at[0], pv_recv.at[h], partner).wait_recv()
        part(h, 0, WINDOW, 256, True)
        part(h, 1, WINDOW, 512, True)
        part(h, 2, WINDOW, 512, True)
        part(h, 2, WINDOW + 512, 256, False)
        part(h, 3, WINDOW, 512, True)
        part(h, 3, WINDOW + 512, 512, False)
        return carry

    lax.fori_loop(0, 2, own, 0)

    def finish(h, u):
        whole = jnp.sum(total[h, u], axis=-1, keepdims=True)
        value = (acc[h, u] / whole).reshape(2, SUB, HEAD)
        stage[h, :, pl.ds(u * SUB, SUB), :] = value.astype(jnp.bfloat16)

    def out_copies(h, j):
        columns = span(core * 4 + h * 2 + j, HEAD)
        local = pltpu.make_async_copy(
            stage.at[h, j, mine_rows], o_hbm.at[:, columns], o_loc.at[h, j]
        )
        away = remote(
            stage.at[h, j, span(other, ROWS)],
            o_hbm.at[:, columns],
            o_send.at[h, j],
            o_recv.at[h, j],
            partner,
        )
        return local, away

    def arrived(buffer, h, s, sems):
        remote(ksend.at[0], buffer.at[h, pl.ds(s * ROWS, ROWS)], k_send.at[0, 0], sems.at[h, s], partner).wait_recv()

    @pl.when(has_before)
    def _():
        for s in range(2):
            arrived(vbuf, 0, s, v_recv)
            arrived(kbuf, 0, s, k_recv)
            if s == 0:
                part(0, 0, 0, 512, False)
                part(0, 1, 256, 256, False)
            else:
                for u in range(4):
                    part(0, u, max(512, u * SUB), WINDOW - max(512, u * SUB), False)

    for u in range(4):
        finish(0, u)
    for j in range(2):
        for copy in out_copies(0, j):
            copy.start()

    @pl.when(has_before)
    def _():
        for s in range(2):
            arrived(kbuf, 1, s, k_recv)
            for u in range(4):
                first, last = max(s * ROWS, u * SUB), (s + 1) * ROWS
                if first < last:
                    weight, lanes = weigh(1, u, first, last - first)
                    held[u, :, pl.ds(first, last - first)] = weight
                    total[1, u] += lanes
        for s in range(2):
            arrived(vbuf, 1, s, v_recv)

    def mix(block):
        for u in (2 * block, 2 * block + 1):
            keys = pl.ds(u * SUB, WINDOW - u * SUB)

            @pl.when(has_before)
            def _():
                acc[1, u] += jnp.dot(held[u, :, keys], vbuf[1, keys, :], preferred_element_type=jnp.float32)

            finish(1, u)

    def last_tiles(first_block):
        mix(first_block)
        for j in range(2):
            out_copies(1, j)[1].start()
        mix(1 - first_block)

    pl.when(core == 0)(lambda: last_tiles(1))
    pl.when(core == 1)(lambda: last_tiles(0))
    for j in range(2):
        out_copies(1, j)[0].start()

    for h in range(2):
        for j in range(2):
            local, away = out_copies(h, j)
            local.wait()
            away.wait_send()
            columns = span(other * 4 + h * 2 + j, HEAD)
            remote(stage.at[h, j, mine_rows], o_hbm.at[:, columns], o_send.at[h, j], o_recv.at[h, j], partner).wait_recv()
    for copy in flag_out[:1] + pv_out + pk_out + q_out:
        copy.wait_send()

    @pl.when(has_after)
    def _():
        for copy in flag_out[1:] + v_out + k_out:
            copy.wait_send()


def solution(mesh):
    count = mesh.shape["ctx"]
    inverse = 10000.0 ** (-(np.arange(HALF, dtype=np.float64) * (2.0 / HEAD)))
    angle = np.arange(ROWS, dtype=np.float64)[:, None] * inverse
    table = np.stack([np.cos(angle), np.sin(angle), 0 * angle + inverse]).astype(np.float32)

    def body(queries, keys, values, query_gain, key_gain, session_flags, valid_length):
        assert queries.shape[0] == ROWS and 2 * ROWS == WINDOW
        pinned = functools.partial(pltpu.with_memory_space_constraint, memory_space=pltpu.HBM)
        bf16, f32, i32 = jnp.bfloat16, jnp.float32, jnp.int32
        dma = pltpu.SemaphoreType.DMA
        anywhere = pl.BlockSpec(memory_space=pltpu.HBM)
        vmem = pl.BlockSpec(memory_space=pltpu.VMEM)
        mixed = pl.pallas_call(
            functools.partial(kernel, count),
            out_shape=pltpu.VMEM((ROWS, QUERY_HEADS * HEAD), bf16),
            in_specs=[anywhere, anywhere, anywhere, vmem, vmem, vmem, anywhere],
            out_specs=pl.BlockSpec(memory_space=pl.ANY),
            scratch_shapes=[
                pltpu.VMEM((ROWS, QUERY_HEADS * HEAD), bf16),
                pltpu.VMEM((ROWS, KEY_VALUE_HEADS * HEAD), bf16),
                pltpu.VMEM((3, ROWS, HALF), f32),
                pltpu.VMEM((2, 4 * ROWS, HEAD), bf16),
                pltpu.VMEM((2, 4 * ROWS, HEAD), bf16),
                pltpu.VMEM((2, ROWS, HEAD), bf16),
                pltpu.VMEM((2, 2, 2 * ROWS, HEAD), bf16),
                pltpu.VMEM((4, ROWS, HEAD), bf16),
                pltpu.VMEM((4, 8, ROWS), i32),
                pltpu.VMEM((2 * ROWS, 128), i32),
                pltpu.VMEM((2, 4, 2 * SUB, HEAD), f32),
                pltpu.VMEM((2, 4, 2 * SUB, 128), f32),
                pltpu.VMEM((2, 2, 2 * ROWS, HEAD), bf16),
                pltpu.VMEM((4, 2 * SUB, WINDOW), bf16),
                dma((3,)),
                dma((2,)),
                dma((3,)),
                dma((3,)),
                dma((2,)),
                dma((2,)),
                dma((2,)),
                dma((2,)),
                dma((2, 2)),
                dma((2, 2)),
                dma((2, 2)),
                dma((2, 2)),
                dma((4,)),
                dma((4,)),
                dma((2, 2)),
                dma((2, 2)),
                dma((2, 2)),
            ],
            compiler_params=pltpu.CompilerParams(
                collective_id=0, has_side_effects=True, vmem_limit_bytes=60 << 20
            ),
        )(
            pinned(queries),
            pinned(keys),
            pinned(values),
            query_gain.reshape(1, HEAD),
            key_gain.reshape(1, HEAD),
            session_flags.reshape(1, ROWS),
            pinned(jnp.asarray(table)),
        )
        tick = lax.axis_index("ctx") * ROWS + lax.broadcasted_iota(i32, mixed.shape, 0)
        return jnp.where(tick < valid_length[0], mixed, jnp.zeros((), bf16))

    return jax.shard_map(
        body,
        mesh=mesh,
        in_specs=(
            P(("dates", "ctx"), None),
            P(("dates", "ctx"), None),
            P(("dates", "ctx"), None),
            P(),
            P(),
            P(("dates", "ctx")),
            P("dates"),
        ),
        out_specs=P(("dates", "ctx"), None),
        check_vma=False,
    )
```
